32 devices in a mesh: cp: 4 (over y, x), fsdp: 2 (over core), rep: 4 (over z).
Axes of the slice: x: 2, y: 2, z: 4, core: 2. Of those that a mesh axis runs over, the one named last changes fastest.
Arguments:
- tokens: bfloat16 [16, 2048, 768], P(('fsdp', 'rep'), 'cp'), may hold values from -6 to 6
- segments: int32 [16, 2048], P(('fsdp', 'rep')), may hold values from 0 to 3, never falling along the last dimension, each value on 1 to 1024 neighbouring positions
- g_one: bfloat16 [768], P('fsdp'), may hold values from 0.099609375 to 1.8984375
- b_one: bfloat16 [768], P('fsdp'), may hold values from -3 to 3
- w_qkv: bfloat16 [768, 2304], P('fsdp'), may hold values from -0.21875 to 0.21875
- b_query: bfloat16 [768], P('fsdp'), may hold values from -3 to 3
- b_value: bfloat16 [768], P('fsdp'), may hold values from -3 to 3
- w_out: bfloat16 [768, 768], P('fsdp'), may hold values from -1.75 to 1.75
- b_out: bfloat16 [768], P('fsdp'), may hold values from -3 to 3
- g_two: bfloat16 [768], P('fsdp'), may hold values from 0.099609375 to 1.8984375
- b_two: bfloat16 [768], P('fsdp'), may hold values from -3 to 3
- w_fc: bfloat16 [768, 3072], P('fsdp'), may hold values from -0.21875 to 0.21875
- b_fc: bfloat16 [3072], P('fsdp'), may hold values from -3 to 3
- w_proj: bfloat16 [3072, 768], P('fsdp'), may hold values from -0.109375 to 0.109375
- b_proj: bfloat16 [768], P('fsdp'), may hold values from -3 to 3
- cotangent: bfloat16 [16, 2048, 768], P(('fsdp', 'rep'), 'cp'), may hold values from -6 to 6
Outputs:
- layer_out: bfloat16 [16, 2048, 768], P(('fsdp', 'rep'), 'cp')
- tokens_grad: bfloat16 [16, 2048, 768], P(('fsdp', 'rep'), 'cp')
- dg_one: float32 [768], P('fsdp')
- db_one: float32 [768], P('fsdp')
- dw_qkv: float32 [768, 2304], P('fsdp')
- db_query: float32 [768], P('fsdp')
- db_value: float32 [768], P('fsdp')
- dw_out: float32 [768, 768], P('fsdp')
- db_out: float32 [768], P('fsdp')
- dg_two: float32 [768], P('fsdp')
- db_two: float32 [768], P('fsdp')
- dw_fc: float32 [768, 3072], P('fsdp')
- db_fc: float32 [3072], P('fsdp')
- dw_proj: float32 [3072, 768], P('fsdp')
- db_proj: float32 [768], P('fsdp')
The draws below stay inside these ranges and needn't reach their ends.
Inputs may be any that keep to these rules, and one draw needn't show every extreme that they name: `segments`: in each sequence the ids never fall, and each document holds 1 to 1024 positions, one document exactly that many.
All inputs are finite; a program needn't handle non-finite values.
Results may differ from the reference program's by a relative error of at most 0.012.
The reference program's roundings to bfloat16 on the way count: a program that leaves them out, or rounds other values in their place, can miss the bound.
Values may be sent and summed in bfloat16 or wider, within the bound.
A program may use at most 384 MiB of HBM per device.

```python
import math
import jax
import jax.numpy as jnp
import numpy as np
from jax import lax

D = 768
HEADS = 12
FF = 3072
SEQ_LEN = 2048
DOCS = 4
SEQS = 16


def block_levels(rng, dims, pieces, least, top_value):
    def one(dim, parts):
        steps = jax.random.uniform(jax.random.fold_in(jax.random.fold_in(rng, 6), dim), (parts,), jnp.float32, least / len(pieces), top_value / len(pieces))
        return jnp.repeat(jnp.exp(steps), dims[dim] // parts).reshape((-1,) + (1,) * (len(dims) - dim - 1))

    factor_of = one(*pieces[0])
    for cut in pieces[1:]:
        factor_of = factor_of * one(*cut)
    return factor_of


def split_up(number_of, total, bound, lean):
    loads = [(1 << 20) // math.isqrt(grade ** lean) + 1 for grade in range(2, number_of + 1)]
    rest, holding = total - bound - (number_of - 1), [1] * (number_of - 1)
    while rest > 0:
        candidates = [i for i in range(number_of - 1) if holding[i] < bound]
        mass, left = sum([loads[i] for i in candidates]), rest
        for i in candidates:
            extra = min(bound - holding[i], max(1, left * loads[i] // mass), rest)
            holding[i] = holding[i] + extra
            rest = rest - extra
    return np.array([bound] + holding)


def ragged_sizes(stream_key, count, total, most, lean):
    if count == 2:
        one = jax.random.randint(stream_key, (), max(1, total - most), min(most, total - 1) + 1)
        return jnp.stack([one, total - one])
    tallies = jnp.asarray(split_up(count, total, most, lean), jnp.int32)
    pairs = (count - 1) // 2
    donor, taker = tallies[1:1 + 2 * pairs:2], tallies[2:2 + 2 * pairs:2]
    room = jnp.minimum(donor - 1, most - taker)
    moved = jax.random.randint(jax.random.fold_in(stream_key, 1), (pairs,), 0, 1 << 20) % (room + 1)
    tallies = tallies.at[1:1 + 2 * pairs:2].set(donor - moved).at[2:2 + 2 * pairs:2].set(taker + moved)
    return tallies[jax.random.permutation(jax.random.fold_in(stream_key, 2), count)]


def bell_draw(key, shape, scale, reach, cuts=(), kind=jnp.bfloat16):
    loudness = block_levels(key, shape, cuts, -0.22, 0.18) if cuts else 1.0
    entries = jax.random.normal(key, shape, jnp.float32) * scale * loudness
    return jnp.minimum(jnp.maximum(entries, -reach), reach).astype(kind)


def setup_inputs(seed: int = 0) -> dict:
    seeds = jax.random.split(jax.random.key(seed), 17)
    tokens = bell_draw(seeds[0], (SEQS, SEQ_LEN, D), 1.0, 6.0, ((0, 8), (1, 4)))
    segments = jax.vmap(lambda own: jnp.searchsorted(jnp.cumsum(ragged_sizes(own, DOCS, SEQ_LEN, SEQ_LEN // 2, 1)), jnp.arange(SEQ_LEN), side="right"))(jax.random.split(seeds[1], SEQS)).reshape((SEQS, SEQ_LEN)).astype(jnp.int32)
    g_one = jnp.clip(1.0 + 0.18 * jax.random.normal(seeds[2], (D,), jnp.float32), 0.099609375, 1.8984375).astype(jnp.bfloat16)
    b_one = bell_draw(seeds[3], (D,), 0.5, 3.0, ((0, 2),))
    w_qkv = bell_draw(seeds[4], (D, 3 * D), D ** -0.5, 0.21875, ((0, 2),))
    b_query = bell_draw(seeds[5], (D,), 0.5, 3.0, ((0, 2),))
    b_value = bell_draw(seeds[6], (D,), 0.5, 3.0, ((0, 2),))
    w_out = bell_draw(seeds[7], (D, D), HEADS ** -0.5, 1.75, ((0, 2),))
    b_out = bell_draw(seeds[8], (D,), 0.5, 3.0, ((0, 2),))
    g_two = jnp.clip(1.0 + 0.18 * jax.random.normal(seeds[9], (D,), jnp.float32), 0.099609375, 1.8984375).astype(jnp.bfloat16)
    b_two = bell_draw(seeds[10], (D,), 0.5, 3.0, ((0, 2),))
    w_fc = bell_draw(seeds[11], (D, FF), D ** -0.5, 0.21875, ((0, 2),))
    b_fc = bell_draw(seeds[12], (FF,), 0.5, 3.0, ((0, 2),))
    w_proj = bell_draw(seeds[13], (FF, D), FF ** -0.5, 0.109375, ((0, 2),))
    b_proj = bell_draw(seeds[14], (D,), 0.5, 3.0, ((0, 2),))
    cotangent = bell_draw(seeds[15], (SEQS, SEQ_LEN, D), 1.0, 6.0, ((0, 8), (1, 4)))
    return {"tokens": tokens, "segments": segments, "g_one": g_one, "b_one": b_one, "w_qkv": w_qkv, "b_query": b_query, "b_value": b_value, "w_out": w_out, "b_out": b_out, "g_two": g_two, "b_two": b_two, "w_fc": w_fc, "b_fc": b_fc, "w_proj": w_proj, "b_proj": b_proj, "cotangent": cotangent}


@jax.custom_vjp
def low(v):
    return lax.optimization_barrier(v.astype(jnp.bfloat16)).astype(jnp.float32)

@jax.custom_vjp
def low_back(v):
    return v

def low_keep(v):
    return (low(v), None)

def low_pass(kept, grad):
    return (grad,)

def back_keep(v):
    return (v, None)

def back_low(kept, grad):
    return (low(grad),)
low.defvjp(low_keep, low_pass)
low_back.defvjp(back_keep, back_low)

def layer_norm(value, gain, shift):
    center = value - lax.optimization_barrier(jnp.mean(value, axis=-1, keepdims=True))
    spread = lax.optimization_barrier(jnp.mean(center * center, axis=-1, keepdims=True))
    return center * lax.rsqrt(spread + 1e-05) * gain + shift

def gelu_tanh(value):
    return 0.5 * value * (1.0 + jnp.tanh(0.7978845608028654 * (value + 0.044715 * value * value * value)))

def matmul(left, right):
    return jnp.dot(left, right, precision=lax.Precision.HIGHEST)

def one_sequence(seq_x, seq_ids, params):
    g_one, b_one, w_qkv, b_query, b_value, w_out, b_out, g_two, b_two, w_fc, b_fc, w_proj, b_proj = params
    width = g_one.shape[0]
    length = seq_x.shape[0]
    size = width // HEADS
    normed = low(layer_norm(seq_x, g_one, b_one))
    merged = matmul(normed, w_qkv) + jnp.concatenate([b_query, jnp.zeros_like(b_query), b_value])
    merged = low(low_back(merged))
    query = merged[:, :width].reshape(length, HEADS, size)
    keys = merged[:, width:2 * width].reshape(length, HEADS, size)
    values = merged[:, 2 * width:].reshape(length, HEADS, size)
    scores = jnp.einsum('qhd,khd->hqk', query, keys, precision=lax.Precision.HIGHEST) * size ** (-0.5)
    scores = low_back(scores)
    places = jnp.arange(length)
    allowed = (seq_ids[:, None] == seq_ids[None, :]) & (places[None, :] <= places[:, None])
    scores = jnp.where(allowed[None], scores, -1e+30)
    top = lax.optimization_barrier(jnp.max(scores, axis=-1, keepdims=True))
    expo = jnp.exp(scores - top)
    probs = low(expo / lax.optimization_barrier(jnp.sum(expo, axis=-1, keepdims=True)))
    mixed = jnp.einsum('hqk,khd->qhd', probs, values, precision=lax.Precision.HIGHEST).reshape(length, width)
    mixed = low(low_back(mixed))
    branch = low_back(matmul(mixed, w_out) + b_out)
    resid = seq_x + branch
    normed_two = low(layer_norm(resid, g_two, b_two))
    hidden = low_back(matmul(normed_two, w_fc) + b_fc)
    active = low(gelu_tanh(hidden))
    output = low_back(matmul(active, w_proj) + b_proj)
    return resid + output

def reference(tokens, segments, g_one, b_one, w_qkv, b_query, b_value, w_out, b_out, g_two, b_two, w_fc, b_fc, w_proj, b_proj, cotangent):
    params = tuple((p.astype(jnp.float32) for p in (g_one, b_one, w_qkv, b_query, b_value, w_out, b_out, g_two, b_two, w_fc, b_fc, w_proj, b_proj)))
    tok_float = tokens.astype(jnp.float32)

    def forward(inputs, weights):

        def each(item):
            return jax.checkpoint(one_sequence)(item[0], item[1], weights)
        return lax.map(each, (inputs, segments))
    result, pullback = jax.vjp(forward, tok_float, params)
    grad_x, grad_p = pullback(cotangent.astype(jnp.float32))
    return (result.astype(jnp.bfloat16), grad_x.astype(jnp.bfloat16), grad_p[0], grad_p[1], grad_p[2], grad_p[3], grad_p[4], grad_p[5], grad_p[6], grad_p[7], grad_p[8], grad_p[9], grad_p[10], grad_p[11], grad_p[12])
```

```python
import jax
import jax.numpy as jnp
from jax import lax
from jax.experimental import pallas as pl
from jax.experimental.pallas import tpu as pltpu
from jax.sharding import PartitionSpec as P

HEADS = 12


def layer_norm(value, gain, shift):
    center = value - jnp.mean(value, axis=-1, keepdims=True)
    spread = jnp.mean(center * center, axis=-1, keepdims=True)
    return center * lax.rsqrt(spread + 1e-05) * gain + shift


def gelu_tanh(value):
    return (
        0.5
        * value
        * (1.0 + jnp.tanh(0.7978845608028654 * (value + 0.044715 * value * value * value)))
    )


def inner_rows(left, right):
    return lax.dot_general(
        left, right, (((0,), (0,)), ((), ())), preferred_element_type=jnp.float32
    )


def times_trans(left, right):
    return lax.dot_general(
        left, right, (((1,), (1,)), ((), ())), preferred_element_type=jnp.float32
    )


BLOCK = 256
NEG = -1e30


def dot_nt(left, right):
    return lax.dot_general(
        left, right, (((1,), (1,)), ((), ())), preferred_element_type=jnp.float32
    )


def dot_tn(left, right):
    return lax.dot_general(
        left, right, (((0,), (0,)), ((), ())), preferred_element_type=jnp.float32
    )


def block_at(ref, index, per, low, high):
    row = pl.multiple_of((index % per) * BLOCK, BLOCK)
    return ref[index // per, pl.ds(row, BLOCK), low:high]


def mask_of(i, j, starts, diagonal):
    near = j * BLOCK + lax.broadcasted_iota(jnp.int32, (BLOCK, BLOCK), 0)
    allowed = near >= starts
    if diagonal:
        mine = i * BLOCK + lax.broadcasted_iota(jnp.int32, (BLOCK, BLOCK), 1)
        allowed = allowed & (near <= mine)
    return allowed


def attend_kernel(low_ref, start_ref, qkv_ref, out_ref, wide_ref, lse_ref, *, heads, size, per):
    seq = pl.program_id(0)
    group = heads * size
    blocks = start_ref.shape[1] // BLOCK
    scale = size ** (-0.5)

    def one_block(i, _):
        cols = pl.ds(pl.multiple_of(i * BLOCK, BLOCK), BLOCK)
        starts = start_ref[:, cols]
        query = [
            block_at(qkv_ref, i, per, h * size, (h + 1) * size) * jnp.bfloat16(scale)
            for h in range(heads)
        ]

        def step(j, carry, diagonal):
            allowed = mask_of(i, j, starts, diagonal)
            state = []
            for h in range(heads):
                keys = block_at(qkv_ref, j, per, group + h * size, group + (h + 1) * size)
                values = block_at(qkv_ref, j, per, 2 * group + h * size, 2 * group + (h + 1) * size)
                scores = jnp.where(allowed, dot_nt(keys, query[h]), NEG)
                best = jnp.max(scores, axis=0, keepdims=True)
                if carry is None:
                    expo = jnp.exp(scores - best)
                    total = jnp.sum(expo, axis=0, keepdims=True)
                    mixed = dot_tn(values, expo.astype(jnp.bfloat16))
                else:
                    top, total, mixed = carry[h]
                    best = jnp.maximum(best, top)
                    shrink = jnp.exp(top - best)
                    expo = jnp.exp(scores - best)
                    total = total * shrink + jnp.sum(expo, axis=0, keepdims=True)
                    mixed = mixed * shrink + dot_tn(values, expo.astype(jnp.bfloat16))
                state.append((best, total, mixed))
            return tuple(state)

        state = step(i, None, True)
        state = lax.fori_loop(low_ref[seq, i], i, lambda j, c: step(j, c, False), state)
        wide = jnp.concatenate([mixed / total for _, total, mixed in state], axis=0)
        wide_ref[:, cols] = wide
        for h in range(heads):
            lse_ref[h : h + 1, cols] = state[h][0] + jnp.log(state[h][1])
        row = pl.multiple_of((i % per) * BLOCK, BLOCK)
        out_ref[i // per, pl.ds(row, BLOCK), :] = wide.T.astype(jnp.bfloat16)
        return 0

    lax.fori_loop(0, blocks, one_block, 0)


def back_kernel(
    low_ref,
    start_ref,
    qkv_ref,
    grad_ref,
    wide_ref,
    lse_ref,
    out_ref,
    dq_ref,
    dk_ref,
    dv_ref,
    *,
    heads,
    size,
    per,
):
    seq = pl.program_id(0)
    group = heads * size
    blocks = start_ref.shape[1] // BLOCK
    scale = size ** (-0.5)

    def one_block(i, _):
        cols = pl.ds(pl.multiple_of(i * BLOCK, BLOCK), BLOCK)
        starts = start_ref[:, cols]
        row = pl.multiple_of((i % per) * BLOCK, BLOCK)
        grad_t = grad_ref[i // per, pl.ds(row, BLOCK), :].astype(jnp.float32).T
        prod = grad_t * wide_ref[:, cols]
        query, grads, lse, delta = [], [], [], []
        for h in range(heads):
            query.append(
                block_at(qkv_ref, i, per, h * size, (h + 1) * size) * jnp.bfloat16(scale)
            )
            grads.append(block_at(grad_ref, i, per, h * size, (h + 1) * size))
            lse.append(lse_ref[h : h + 1, cols])
            delta.append(jnp.sum(prod[h * size : (h + 1) * size], axis=0, keepdims=True))

        def step(j, carry, diagonal):
            allowed = mask_of(i, j, starts, diagonal)
            rows = pl.ds(pl.multiple_of(j * BLOCK, BLOCK), BLOCK)
            state = []
            for h in range(heads):
                keys = block_at(qkv_ref, j, per, group + h * size, group + (h + 1) * size)
                values = block_at(qkv_ref, j, per, 2 * group + h * size, 2 * group + (h + 1) * size)
                scores = jnp.where(allowed, dot_nt(keys, query[h]), NEG)
                probs = jnp.exp(scores - lse[h])
                d_probs = dot_nt(values, grads[h])
                d_scores = (probs * (d_probs - delta[h])).astype(jnp.bfloat16)
                d_value = jnp.dot(
                    probs.astype(jnp.bfloat16), grads[h], preferred_element_type=jnp.float32
                )
                d_key = jnp.dot(d_scores, query[h], preferred_element_type=jnp.float32)
                d_query = dot_tn(keys, d_scores)
                if diagonal:
                    dk_ref[h, rows, :] = d_key
                    dv_ref[h, rows, :] = d_value
                    state.append(d_query)
                else:
                    dk_ref[h, rows, :] += d_key
                    dv_ref[h, rows, :] += d_value
                    state.append(carry[h] + d_query)
            return tuple(state)

        state = step(i, None, True)
        state = lax.fori_loop(low_ref[seq, i], i, lambda j, c: step(j, c, False), state)
        dq_ref[:, cols] = jnp.concatenate(state, axis=0) * scale
        return 0

    lax.fori_loop(0, blocks, one_block, 0)

    def finish(i, _):
        cols = pl.ds(pl.multiple_of(i * BLOCK, BLOCK), BLOCK)
        row = pl.multiple_of((i % per) * BLOCK, BLOCK)
        parts = [dq_ref[:, cols].T.astype(jnp.bfloat16)]
        parts += [dk_ref[h, cols, :].astype(jnp.bfloat16) for h in range(heads)]
        parts += [dv_ref[h, cols, :].astype(jnp.bfloat16) for h in range(heads)]
        out_ref[i // per, pl.ds(row, BLOCK), :] = jnp.concatenate(parts, axis=1)
        return 0

    lax.fori_loop(0, blocks, finish, 0)


def attend(low, starts, qkv, heads, size):
    ways, seqs, span, three = qkv.shape
    length = ways * span
    group = heads * size
    part = lambda cols: pl.BlockSpec((ways, None, span, cols), lambda s, low: (0, s, 0, 0))
    rows = lambda count: pl.BlockSpec((None, count, length), lambda s, low: (s, 0, 0))
    return pl.pallas_call(
        lambda *refs: attend_kernel(*refs, heads=heads, size=size, per=span // BLOCK),
        name="attend",
        out_shape=(
            jax.ShapeDtypeStruct((ways, seqs, span, group), jnp.bfloat16),
            jax.ShapeDtypeStruct((seqs, group, length), jnp.float32),
            jax.ShapeDtypeStruct((seqs, heads, length), jnp.float32),
        ),
        grid_spec=pltpu.PrefetchScalarGridSpec(
            num_scalar_prefetch=1,
            grid=(seqs,),
            in_specs=[rows(1), part(three)],
            out_specs=[part(group), rows(group), rows(heads)],
        ),
        compiler_params=pltpu.CompilerParams(
            dimension_semantics=("arbitrary",), vmem_limit_bytes=40 << 20
        ),
        cost_estimate=pl.CostEstimate(
            flops=20_000_000_000, bytes_accessed=12_000_000, transcendentals=10_000_000
        ),
    )(low, starts, qkv)


def attend_back(low, starts, qkv, grad, wide, lse, heads, size):
    ways, seqs, span, three = qkv.shape
    length = ways * span
    group = heads * size
    part = lambda cols: pl.BlockSpec((ways, None, span, cols), lambda s, low: (0, s, 0, 0))
    rows = lambda count: pl.BlockSpec((None, count, length), lambda s, low: (s, 0, 0))
    return pl.pallas_call(
        lambda *refs: back_kernel(*refs, heads=heads, size=size, per=span // BLOCK),
        name="attend_back",
        out_shape=jax.ShapeDtypeStruct((ways, seqs, span, three), jnp.bfloat16),
        grid_spec=pltpu.PrefetchScalarGridSpec(
            num_scalar_prefetch=1,
            grid=(seqs,),
            in_specs=[rows(1), part(three), part(group), rows(group), rows(heads)],
            out_specs=part(three),
            scratch_shapes=[
                pltpu.VMEM((group, length), jnp.float32),
                pltpu.VMEM((heads, length, size), jnp.float32),
                pltpu.VMEM((heads, length, size), jnp.float32),
            ],
        ),
        compiler_params=pltpu.CompilerParams(
            dimension_semantics=("arbitrary",), vmem_limit_bytes=48 << 20
        ),
        cost_estimate=pl.CostEstimate(
            flops=50_000_000_000, bytes_accessed=18_000_000, transcendentals=10_000_000
        ),
    )(low, starts, qkv, grad, wide, lse)


def swap(value):
    return lax.all_to_all(value, "cp", 0, 0, tiled=True)


def body(
    tokens,
    segments,
    g_one,
    b_one,
    w_qkv,
    b_query,
    b_value,
    w_out,
    b_out,
    g_two,
    b_two,
    w_fc,
    b_fc,
    w_proj,
    b_proj,
    cotangent,
):
    seqs, span, width = tokens.shape
    rows = seqs * span
    size = width // HEADS
    ways = lax.axis_size("cp")
    heads = HEADS // ways
    group = heads * size

    vectors = (g_one, b_one, b_query, b_value, b_out, g_two, b_two, b_proj, b_fc)
    packed = lax.all_gather(jnp.concatenate(vectors), "fsdp", axis=0)
    vecs, at = [], 0
    for vector in vectors:
        vecs.append(packed[:, at : at + vector.shape[0]].reshape(-1).astype(jnp.float32))
        at += vector.shape[0]
    gain_one, shift_one, bias_q, bias_v, bias_out, gain_two, shift_two, bias_proj, bias_fc = vecs
    full_qkv = lax.all_gather(w_qkv, "fsdp", axis=0, tiled=True)
    full_out = lax.all_gather(w_out, "fsdp", axis=0, tiled=True)
    full_fc = lax.all_gather(w_fc, "fsdp", axis=0, tiled=True)
    full_proj = lax.all_gather(w_proj, "fsdp", axis=0, tiled=True)

    starts = sum(
        jnp.where(segments > v, jnp.sum(segments == v, axis=1, keepdims=True), 0)
        for v in range(3)
    ).astype(jnp.int32)
    low = starts[:, ::BLOCK] // BLOCK
    starts = starts[:, None, :]

    tok_rows = tokens.reshape(rows, width).astype(jnp.float32)
    normed = layer_norm(tok_rows, gain_one, shift_one).astype(jnp.bfloat16)
    qkv_bias = jnp.concatenate([bias_q, jnp.zeros_like(bias_q), bias_v])
    merged = (jnp.dot(normed, full_qkv, preferred_element_type=jnp.float32) + qkv_bias).astype(
        jnp.bfloat16
    )
    merged = merged.reshape(rows, 3, ways, group).transpose(2, 0, 1, 3)
    qkv = swap(merged.reshape(ways, seqs, span, 3 * group))
    mixed, wide, lse = attend(low, starts, qkv, heads, size)
    mixed_rows = swap(mixed).reshape(ways, rows, group).transpose(1, 0, 2).reshape(rows, width)

    branch = jnp.dot(mixed_rows, full_out, preferred_element_type=jnp.float32) + bias_out
    resid = tok_rows + branch
    normed_two = layer_norm(resid, gain_two, shift_two).astype(jnp.bfloat16)
    hidden = jnp.dot(normed_two, full_fc, preferred_element_type=jnp.float32) + bias_fc
    active = gelu_tanh(hidden).astype(jnp.bfloat16)
    output = jnp.dot(active, full_proj, preferred_element_type=jnp.float32) + bias_proj
    layer_out = (resid + output).astype(jnp.bfloat16).reshape(seqs, span, width)

    d_output = cotangent.reshape(rows, width)
    out_grad = d_output.astype(jnp.float32)
    db_proj = jnp.sum(out_grad, axis=0)
    d_active = times_trans(d_output, full_proj)
    _, gelu_pull = jax.vjp(gelu_tanh, hidden)
    d_hidden = gelu_pull(d_active)[0].astype(jnp.bfloat16)
    db_fc = jnp.sum(d_hidden.astype(jnp.float32), axis=0)
    d_normed_two = times_trans(d_hidden, full_fc)
    _, norm_pull_two = jax.vjp(layer_norm, resid, gain_two, shift_two)
    d_resid_part, dg_two, db_two = norm_pull_two(d_normed_two)
    d_resid = out_grad + d_resid_part
    d_branch = d_resid.astype(jnp.bfloat16)
    db_out = jnp.sum(d_branch.astype(jnp.float32), axis=0)
    d_mixed = times_trans(d_branch, full_out).astype(jnp.bfloat16)
    d_mixed = (
        d_mixed.reshape(rows, ways, group).transpose(1, 0, 2).reshape(ways, seqs, span, group)
    )

    def scattered(grad):
        return lax.psum_scatter(grad, "fsdp", scatter_dimension=0, tiled=True)

    dw_proj = scattered(inner_rows(active, d_output).astype(jnp.bfloat16))
    dw_fc = scattered(inner_rows(normed_two, d_hidden).astype(jnp.bfloat16))
    d_mixed = swap(d_mixed)

    d_qkv = swap(attend_back(low, starts, qkv, d_mixed, wide, lse, heads, size))
    d_merged = (
        d_qkv.reshape(ways, rows, 3, group).transpose(1, 2, 0, 3).reshape(rows, 3 * width)
    )
    dw_qkv = scattered(inner_rows(normed, d_merged).astype(jnp.bfloat16))
    d_merged_sum = jnp.sum(d_merged.astype(jnp.float32), axis=0)
    db_query = d_merged_sum[:width]
    db_value = d_merged_sum[2 * width :]
    d_normed = times_trans(d_merged, full_qkv)
    _, norm_pull_one = jax.vjp(layer_norm, tok_rows, gain_one, shift_one)
    d_tok_part, dg_one, db_one = norm_pull_one(d_normed)
    tokens_grad = (d_resid + d_tok_part).astype(jnp.bfloat16).reshape(seqs, span, width)

    small = (dg_one, db_one, db_query, db_value, db_out, dg_two, db_two, db_proj, db_fc)
    shards = lax.axis_size("fsdp")
    flat = jnp.concatenate([grad.reshape(shards, -1) for grad in small], axis=1)
    count = flat.shape[1]
    extra = 16 * pl.cdiv(count, 16 * width)
    flat = jnp.pad(flat, ((0, 0), (0, extra * width - count))).reshape(shards, extra, width)
    dw_out = inner_rows(mixed_rows, d_branch).reshape(shards, -1, width)
    both = jnp.concatenate([dw_out, flat], axis=1).reshape(-1, width)
    both = scattered(both.astype(jnp.bfloat16))
    sums = lax.psum((dw_qkv, both, dw_fc, dw_proj), ("cp", "rep"))
    dw_qkv, both, dw_fc, dw_proj = [part.astype(jnp.float32) for part in sums]
    dw_out, flat = both[: width // shards], both[width // shards :].reshape(-1)
    own, at = [], 0
    for vector in vectors:
        own.append(flat[at : at + vector.shape[0]])
        at += vector.shape[0]
    dg_one, db_one, db_query, db_value, db_out, dg_two, db_two, db_proj, db_fc = own
    return (
        layer_out,
        tokens_grad,
        dg_one,
        db_one,
        dw_qkv,
        db_query,
        db_value,
        dw_out,
        db_out,
        dg_two,
        db_two,
        dw_fc,
        db_fc,
        dw_proj,
        db_proj,
    )


def solution(mesh):
    placed = (
        P(("fsdp", "rep"), "cp", None),
        P(("fsdp", "rep"), None),
        P("fsdp"),
        P("fsdp"),
        P("fsdp", None),
        P("fsdp"),
        P("fsdp"),
        P("fsdp", None),
        P("fsdp"),
        P("fsdp"),
        P("fsdp"),
        P("fsdp", None),
        P("fsdp"),
        P("fsdp", None),
        P("fsdp"),
        P(("fsdp", "rep"), "cp", None),
    )
    return jax.shard_map(
        body,
        mesh=mesh,
        in_specs=placed,
        out_specs=(
            P(("fsdp", "rep"), "cp", None),
            P(("fsdp", "rep"), "cp", None),
            P("fsdp"),
            P("fsdp"),
            P("fsdp", None),
            P("fsdp"),
            P("fsdp"),
            P("fsdp", None),
            P("fsdp"),
            P("fsdp"),
            P("fsdp"),
            P("fsdp", None),
            P("fsdp"),
            P("fsdp", None),
            P("fsdp"),
        ),
        check_vma=False,
    )
```
